32 devices in a mesh: dens: 2 (over core), sp: 16 (over z, y, x).
Axes of the slice: x: 2, y: 2, z: 4, core: 2. Of those that a mesh axis runs over, the one named last changes fastest.
Arguments:
- densities: float32 [2, 64, 512, 512], P('dens', 'sp'), may hold values from 0.2 to 5
- weights: float32 [2], P('dens'), may hold values from 0.5 to 2
- spreads: float32 [3], replicated, may hold values from 1 to 3.2, as said below
Outputs:
- barycenter: float32 [64, 512, 512], P('sp')
- scalings: float32 [2, 64, 512, 512], P('dens', 'sp')
The draws below stay inside these ranges and needn't reach their ends.
Inputs may be any that keep to these rules, and one draw needn't show every extreme that they name: The vertical width spreads[0] lies within 2.4 to 3.2 cells, the two horizontal widths within 1.0 to 2.5 cells.
All inputs are finite; a program needn't handle non-finite values.
Results may differ from the reference program's by a relative error of at most 0.0001.
Values sent between devices are 32-bit elements; how exact they have to be, the bound alone decides.
No kernel may reach another device: no remote copies, remote signals or barrier semaphores. Data moves between devices by JAX's collectives and lax.ppermute only.
A program may use at most 128 MiB of HBM per device.

```python
import math
import jax
import jax.numpy as jnp
from jax import lax

NX = 512
NY = 512
NZ = 64
ITERS = 2
DENS = 2


def draw_spreads(key, part):
    uniform_part = jax.random.uniform(jax.random.fold_in(key, 17), (3,), jnp.float32)
    lower = jnp.array([2.4, 1.0, 1.0], jnp.float32)
    upper = jnp.array([3.2, 2.5, 2.5], jnp.float32)
    return jnp.exp(jnp.log(lower) + uniform_part * (jnp.log(upper) - jnp.log(lower)))


def level_of(key, extent, split, low, largest):
    def one(position, shards_of):
        heights = jax.random.uniform(jax.random.fold_in(jax.random.fold_in(key, 6), position), (shards_of,), jnp.float32, low / len(split), largest / len(split))
        return jnp.repeat(jnp.exp(heights), extent[position] // shards_of).reshape((-1,) + (1,) * (len(extent) - position - 1))

    factor_of = one(*split[0])
    for cut in split[1:]:
        factor_of = factor_of * one(*cut)
    return factor_of


def setup_inputs(seed: int = 0) -> dict:
    key_of = jax.random.split(jax.random.key(seed), 4)
    densities = jnp.clip(jnp.exp(math.log(5.0) - 3.218876 * jax.random.uniform(key_of[0], (DENS, NZ, NX, NY), jnp.float32) ** level_of(key_of[0], (DENS, NZ, NX, NY), ((0, 2), (1, 16)), -0.2, 0.2)), 0.2, 5.0)
    weights = jnp.clip(jnp.exp(math.log(2.0) - 1.3862944 * jax.random.uniform(key_of[1], (DENS,), jnp.float32) ** level_of(key_of[1], (DENS,), ((0, 2),), -0.2, 0.2)), 0.5, 2.0)
    spreads = draw_spreads(jax.random.fold_in(key_of[3], 71), 0)
    return {"densities": densities, "weights": weights, "spreads": spreads}


def kernel_matrix(length, spread):
    pos = jnp.arange(length).astype(jnp.float32)
    diff = (pos[:, None] - pos[None, :]) / spread
    return jnp.exp(-diff * diff) / (spread * jnp.sqrt(jnp.float32(jnp.pi)))

def convolve(field, kern_z, kern_x, kern_y):
    hp = lax.Precision.HIGHEST
    field = jnp.einsum('zxy,yk->zxk', field, kern_y, precision=hp)
    field = jnp.einsum('zxy,xk->zky', field, kern_x, precision=hp)
    return jnp.einsum('zxy,zk->kxy', field, kern_z, precision=hp)

def reference(densities, weights, spreads):
    kern_z = kernel_matrix(NZ, spreads[0])
    kern_x = kernel_matrix(NX, spreads[1])
    kern_y = kernel_matrix(NY, spreads[2])
    alpha = weights / jnp.sum(weights)

    def conv_all(stack):
        return lax.map(lambda f: convolve(f, kern_z, kern_x, kern_y), stack)
    scale_v = jnp.ones_like(densities)
    scale_w = scale_v
    barycenter = None
    for step in range(ITERS):
        scale_w = densities / conv_all(scale_v)
        marginal = scale_v * conv_all(scale_w)
        logbar = lax.optimization_barrier(jnp.sum(alpha[:, None, None, None] * jnp.log(marginal), axis=0))
        barycenter = jnp.exp(logbar)
        scale_v = scale_v * barycenter[None] / marginal
    return (barycenter, scale_w)
```

```python
import jax
import jax.numpy as jnp
from jax import lax
from jax.sharding import PartitionSpec as P

ITERS = 2
PREC = lax.Precision.HIGH


def kernel_matrix(length, spread):
    pos = jnp.arange(length).astype(jnp.float32)
    diff = (pos[:, None] - pos[None, :]) / spread
    return jnp.exp(-diff * diff) / (spread * jnp.sqrt(jnp.float32(jnp.pi)))


def along_planes(field, kern_x, kern_y):
    field = jnp.einsum("zxy,yk->zxk", field, kern_y, precision=PREC)
    return jnp.einsum("zxy,xk->zky", field, kern_x, precision=PREC)


def along_columns(field, kern_z):
    return jnp.einsum("zxy,zk->kxy", field, kern_z, precision=PREC)


def to_columns(field):
    return lax.all_to_all(field, "sp", split_axis=1, concat_axis=0, tiled=True)


def to_planes(field):
    return lax.all_to_all(field, "sp", split_axis=0, concat_axis=1, tiled=True)


def dens_sum(value):
    n = lax.axis_size("dens")
    if n == 2:
        return value + lax.ppermute(value, "dens", [(0, 1), (1, 0)])
    return lax.psum(value, "dens")


def bary_out(term, planes):
    n = lax.axis_size("dens")
    if n != 2 or planes % 2:
        return to_planes(jnp.exp(dens_sum(term)))
    core = lax.axis_index("dens")
    swap = [(0, 1), (1, 0)]
    nz, nx, ny = term.shape
    halves = term.reshape(nz // planes, 2, planes // 2, nx, ny)
    mine = lax.dynamic_index_in_dim(halves, core, 1, keepdims=False)
    other = lax.dynamic_index_in_dim(halves, 1 - core, 1, keepdims=False)
    summed = mine + lax.ppermute(other, "dens", swap)
    half = to_planes(jnp.exp(summed).reshape(nz // 2, nx, ny))
    rest = lax.ppermute(half, "dens", swap)
    first = jnp.where(core == 0, half, rest)
    second = jnp.where(core == 0, rest, half)
    return jnp.concatenate([first, second], axis=0)


def local(densities, weights, spreads):
    planes = densities.shape[1]
    nz = planes * lax.axis_size("sp")
    nx = densities.shape[2]
    ny = densities.shape[3]
    kern_z = kernel_matrix(nz, spreads[0])
    kern_x = kernel_matrix(nx, spreads[1])
    kern_y = kernel_matrix(ny, spreads[2])
    alpha = weights[0] / dens_sum(weights[0])
    target = densities[0]

    def first(kern):
        return kern / jnp.sum(kern, axis=0)[:, None]

    columns = to_columns(along_planes(target, first(kern_x), first(kern_y)))
    marginal = along_columns(columns, first(kern_z))
    scale_w = target
    scale_v = None
    for step in range(1, ITERS):
        term = alpha * jnp.log(marginal)
        barycenter = jnp.exp(dens_sum(term))
        scale_v = barycenter / marginal if scale_v is None else scale_v * barycenter / marginal
        blurred_v = along_planes(to_planes(along_columns(scale_v, kern_z)), kern_x, kern_y)
        scale_w = target / blurred_v
        columns = to_columns(along_planes(scale_w, kern_x, kern_y))
        marginal = scale_v * along_columns(columns, kern_z)
    barycenter = bary_out(alpha * jnp.log(marginal), planes)
    return (barycenter, scale_w[None])


def solution(mesh):
    return jax.shard_map(
        local,
        mesh=mesh,
        in_specs=(P("dens", "sp", None, None), P("dens"), P()),
        out_specs=(P("sp", None, None), P("dens", "sp", None, None)),
        check_vma=False,
    )
```

```python
import functools

import jax
import jax.numpy as jnp
import numpy as np
from jax import lax
from jax.experimental import pallas as pl
from jax.experimental.pallas import tpu as pltpu
from jax.sharding import PartitionSpec as P


LANES = 128
TILE = 256
REACH = 32
F32 = jnp.float32
BF16 = jnp.bfloat16


def gauss(diff, spread):
    scaled = diff / spread
    return jnp.exp(-scaled * scaled) / (spread * jnp.sqrt(jnp.float32(jnp.pi)))


def split(value):
    high = value.astype(BF16)
    return high, (value - high.astype(F32)).astype(BF16)


def dot(a, b):
    return jnp.dot(a, b, preferred_element_type=F32)


def call(body, grid, in_specs, out_specs, out_shape, flops=0, moved=0, prefetch=0, scratch=()):
    return pl.pallas_call(
        body,
        grid_spec=pltpu.PrefetchScalarGridSpec(
            num_scalar_prefetch=prefetch,
            grid=grid,
            in_specs=in_specs,
            out_specs=out_specs,
            scratch_shapes=scratch,
        ),
        out_shape=out_shape,
        compiler_params=pltpu.CompilerParams(vmem_limit_bytes=56 << 20),
        cost_estimate=pl.CostEstimate(flops=flops, bytes_accessed=moved, transcendentals=0),
    )


def whole(array):
    return pl.BlockSpec(array.shape, lambda *_: (0,) * array.ndim)


def windows(length, tile, margin):
    tile = min(tile, length)
    return [
        (t, t + tile, max(t - margin, 0), min(t + tile + margin, length))
        for t in range(0, length, tile)
    ]


def row_windows(nx):
    return windows(nx, nx // 2, REACH)


def lane_windows(ny):
    return windows(ny, TILE, LANES)


def count(shape, dim, first=0):
    return (lax.broadcasted_iota(jnp.int32, shape, dim) + first).astype(F32)


def weights_body(nx, ny, spread_ref, hrow_ref, hcol_ref, brow_ref, bcol_ref, *refs):
    refs = list(refs)
    rows_ref = refs.pop(0)
    for t, (start, stop, low, high) in enumerate(row_windows(nx)):
        shape = (stop - start, high - low)
        top, rest = split(gauss(count(shape, 0, start) - count(shape, 1, low), spread_ref[1]))
        rows_ref[t] = jnp.concatenate([top, top, rest], 1)
    for start, stop, low, high in lane_windows(ny):
        shape = (high - low, stop - start)
        top, rest = split(gauss(count(shape, 0, low) - count(shape, 1, start), spread_ref[2]))
        refs.pop(0)[...] = jnp.concatenate([top, top, rest], 0)
    halves_ref, blocks_ref, z_ref, x_ref, y_ref = refs
    nz = z_ref.shape[1]
    shape = (nz, nz)
    spread = spread_ref[0]
    for ref, diff in (
        (halves_ref, hcol_ref[...] - brow_ref[...]),
        (blocks_ref, bcol_ref[...] - hrow_ref[...]),
    ):
        top, rest = split(gauss(diff, spread))
        ref[...] = jnp.concatenate([top, top, rest], 1)
    z_ref[...] = 1.0 / jnp.sum(
        gauss(count(shape, 0) - count(shape, 1), spread), axis=0, keepdims=True
    )
    for ref, axis, length, k in ((x_ref, 1, nx, 1), (y_ref, 0, ny, 2)):
        diff = count((length, length), 0) - count((length, length), 1)
        ref[...] = 1.0 / jnp.sum(gauss(diff, spread_ref[k]), axis=axis, keepdims=True)


def all_weights(spreads, nx, ny, halves, blocks):
    nz = halves.size
    start, stop, low, high = row_windows(nx)[0]
    shapes = [((2, stop - start, 3 * (high - low)), BF16)]
    shapes += [((3 * (h - l), e - s), BF16) for s, e, l, h in lane_windows(ny)]
    shapes += [((nz, 3 * nz), BF16)] * 2 + [((1, nz), F32), ((nx, 1), F32), ((1, ny), F32)]
    out = [jax.ShapeDtypeStruct(*s) for s in shapes]
    ins = [part for order in (halves, blocks) for part in (order[None, :], order[:, None])]
    got = call(
        functools.partial(weights_body, nx, ny),
        (1,),
        [whole(v) for v in ins],
        [whole(s) for s in out],
        out,
        prefetch=1,
    )(spreads, *ins)
    return got[:-5], got[-5:-3], got[-3:]


def blur_tile(field, row_mat, lane_refs, store):
    hi, lo = split(field)
    for (first, last, low, high), lane_ref in zip(lane_windows(field.shape[1]), lane_refs):
        lhs = jnp.concatenate([hi[:, low:high], lo[:, low:high], hi[:, low:high]], 1)
        g_hi, g_lo = split(dot(lhs, lane_ref[...]))
        store(slice(first, last), dot(row_mat, jnp.concatenate([g_hi, g_lo, g_hi], 0)))


def row_start(nx, tile):
    return pl.multiple_of(tile * row_windows(nx)[1][2], 8)


def row_size(nx):
    return row_windows(nx)[0][3]


def give_blocks(device, far, tile_ref, refs):
    n2 = len(refs) // 2 if far else len(refs)
    for k in range(n2):
        rows = refs[k].shape[1] * (2 if far else 1)
        at = pl.multiple_of(((device ^ k) & (n2 - 1)) * rows, 8)
        if far:
            refs[k][0] = tile_ref[pl.ds(at, rows // 2), :]
            refs[n2 + k][0] = tile_ref[pl.ds(at + rows // 2, rows // 2), :]
        else:
            refs[k][0] = tile_ref[pl.ds(at, rows), :]


def tile_body(far, scaled, n_lanes, device_ref, f_ref, *refs):
    _, nx, _ = f_ref.shape
    refs = list(refs)
    device = device_ref[0]
    half = device // device_ref[1]
    tile = 1 - half if far else half
    window = pl.ds(row_start(nx, tile), row_size(nx))
    field = f_ref[0, window, :]
    if scaled:
        z_ref, x_ref, y_ref = refs[:3]
        refs = refs[3:]
        plane = device * pl.num_programs(0) + pl.program_id(0)
        at = lax.broadcasted_iota(jnp.int32, z_ref.shape, 1) == plane
        scale = jnp.sum(jnp.where(at, z_ref[...], 0.0), axis=1, keepdims=True)
        field = field * x_ref[window, :] * (y_ref[...] * scale)
    rows_ref, lane_refs, outs, tile_ref = refs[0], refs[1 : 1 + n_lanes], refs[1 + n_lanes : -1], refs[-1]

    def store(lanes, value):
        tile_ref[:, lanes] = value

    blur_tile(field, rows_ref[tile], lane_refs, store)
    give_blocks(device, far, tile_ref, outs)


def second_body(n_in, n_lanes, device_ref, t_ref, *refs):
    _, nx, _ = t_ref.shape
    blocks, refs = refs[:n_in], refs[n_in:]
    rows_ref, lane_refs, refs = refs[0], refs[1 : 1 + n_lanes], refs[1 + n_lanes :]
    w_ref, outs, field_ref, tile_ref = refs[0], refs[1:-2], refs[-2], refs[-1]
    device = device_ref[0]
    n2 = n_in // 3
    rows = blocks[0].shape[1]
    for k in range(n2):
        field_ref[pl.ds(pl.multiple_of((device ^ k) * rows, 8), rows), :] = blocks[k][0]
        at = pl.multiple_of((device ^ (n2 + k)) * rows, 8)
        field_ref[pl.ds(at, rows // 2), :] = blocks[n2 + k][0]
        field_ref[pl.ds(at + rows // 2, rows // 2), :] = blocks[2 * n2 + k][0]
    for t, (start, stop, low, high) in enumerate(row_windows(nx)):

        def store_w(lanes, value):
            w_ref[0, start:stop, lanes] = t_ref[0, start:stop, lanes] / value

        blur_tile(field_ref[low:high], rows_ref[t], lane_refs, store_w)
    tile = 1 - device // device_ref[1]

    def store(lanes, value):
        tile_ref[:, lanes] = value

    field = w_ref[0, pl.ds(row_start(nx, tile), row_size(nx)), :]
    blur_tile(field, rows_ref[tile], lane_refs, store)
    give_blocks(device, True, tile_ref, outs)


def plane_spec(field):
    return pl.BlockSpec((1,) + field.shape[1:], lambda k, *_: (k, 0, 0))


def far_shapes(planes, n, rows, ny):
    return [jax.ShapeDtypeStruct((planes, rows // 2, ny), F32)] * n


def near_shapes(planes, n, rows, ny):
    return [jax.ShapeDtypeStruct((planes, rows, ny), F32)] * (n // 2)


def blur_part(field, far, device, n, mats, inverses=()):
    planes, nx, ny = field.shape
    out = (far_shapes if far else near_shapes)(planes, n, nx // n, ny)
    return call(
        functools.partial(tile_body, far, bool(inverses), len(mats) - 1),
        (planes,),
        [plane_spec(field), *map(whole, inverses), *map(whole, mats)],
        [plane_spec(o) for o in out],
        out,
        flops=6 * field.size * TILE,
        moved=6 * field.size,
        prefetch=1,
        scratch=[pltpu.VMEM((nx // 2, ny), F32)],
    )(device, field, *inverses, *mats)


def blur_second(blocks, target, device, n, mats):
    planes, nx, ny = target.shape
    out = [jax.ShapeDtypeStruct(target.shape, F32), *far_shapes(planes, n, nx // n, ny)]
    w, *far = call(
        functools.partial(second_body, len(blocks), len(mats) - 1),
        (planes,),
        [plane_spec(target), *map(plane_spec, blocks), *map(whole, mats)],
        [plane_spec(o) for o in out],
        out,
        flops=18 * target.size * TILE,
        moved=14 * target.size,
        prefetch=1,
        scratch=[pltpu.VMEM((nx, ny), F32), pltpu.VMEM((nx // 2, ny), F32)],
    )(device, target, *blocks, *mats)
    return w, far


def z_blur(m_ref, column_of, store, rows):
    for x in range(0, rows, 2):
        cols = []
        for k in (x, x + 1):
            hi, lo = split(column_of(k))
            cols.append(jnp.concatenate([hi, lo, hi], 0))
        both = dot(m_ref[...], jnp.concatenate(cols, 1))
        store(x, both[:, :LANES])
        store(x + 1, both[:, LANES:])


def rows_of(ref, x):
    planes, bx, _ = ref.shape
    return ref.reshape(planes * bx, LANES)[pl.ds(x, planes, stride=bx), :]


def put_rows(ref, x, value):
    planes, bx, _ = ref.shape
    ref.reshape(planes * bx, LANES)[pl.ds(x, planes, stride=bx), :] = value


def gather(blocks, field_ref):
    planes = blocks[0].shape[0]
    for k, block in enumerate(blocks):
        field_ref[k * planes : (k + 1) * planes] = block[...]


def spread_out(field_ref, part, befores, refs):
    n2 = len(refs) // 2
    planes, hr, _ = refs[-1].shape
    for k, ref in enumerate(refs):
        value = field_ref[k * planes : (k + 1) * planes]
        if k < n2 and part == 1:
            ref[:, :hr] = befores[k][...]
            ref[:, hr:] = value
        else:
            ref[...] = value


def log_body(n, *refs):
    blocks, m_ref, l_ref, field_ref = refs[:n], refs[n], refs[n + 1], refs[n + 2]
    gather(blocks, field_ref)

    def store(x, value):
        put_rows(l_ref, x, jnp.log(value))

    z_blur(m_ref, lambda x: rows_of(field_ref, x), store, l_ref.shape[1])


def scale_body(part, n, alpha_ref, l_ref, o_ref, *refs):
    n_before = n // 2 if part else 0
    befores, m_ref, v_ref = refs[:n_before], refs[n_before], refs[n_before + 1]
    outs, field_ref = refs[n_before + 2 : -1], refs[-1]
    logs = l_ref[...]
    v_ref[...] = jnp.exp(alpha_ref[0] * logs + alpha_ref[1] * o_ref[...] - logs)

    def store(x, value):
        put_rows(field_ref, x, value)

    z_blur(m_ref, lambda x: rows_of(v_ref, x), store, l_ref.shape[1])
    spread_out(field_ref, part, befores, outs)


def last_body(n, core_ref, v_ref, *refs):
    blocks, m_ref, mine_ref, send_ref, field_ref = refs[:n], *refs[n:]
    nz, hr, _ = v_ref.shape
    gather(blocks, field_ref)

    def run(out):
        def store(x, value):
            value = jnp.log(rows_of(v_ref, x) * value)
            put_rows(out[0], x, value[: nz // 2])
            put_rows(out[1], x, value[nz // 2 :])

        z_blur(m_ref, lambda x: rows_of(field_ref, x), store, hr)

    @pl.when(core_ref[0] == 0)
    def _():
        run((mine_ref, send_ref))

    @pl.when(core_ref[0] != 0)
    def _():
        run((send_ref, mine_ref))


def exp_body(part, n, alpha_ref, mine_ref, other_ref, *refs):
    n_before = n // 2 if part else 0
    befores, outs, field_ref = refs[:n_before], refs[n_before:-1], refs[-1]
    field_ref[...] = jnp.exp(alpha_ref[0] * mine_ref[...] + alpha_ref[1] * other_ref[...])
    spread_out(field_ref, part, befores, outs)


def columns(body, part, scalars, fields, mats, out_shape, scratch_planes, rows):
    hr = rows // 2

    def spec(s):
        if s.shape[1] == hr:
            return pl.BlockSpec((s.shape[0], hr, LANES), lambda i, *_: (0, 0, i))
        return pl.BlockSpec((s.shape[0], hr, LANES), lambda i, *_: (0, part, i))

    def out_spec(s):
        return pl.BlockSpec((s.shape[0], s.shape[1], LANES), lambda i, *_: (0, 0, i))

    ny = fields[0].shape[2]
    planes = sum(f.shape[0] for f in fields) + sum(s.shape[0] for s in out_shape)
    return call(
        body,
        (ny // LANES,),
        [*map(spec, fields), *map(whole, mats)],
        [out_spec(s) for s in out_shape],
        out_shape,
        flops=12 * scratch_planes * scratch_planes * hr * ny,
        moved=planes * hr * ny * 4,
        prefetch=len(scalars),
        scratch=[pltpu.VMEM((scratch_planes, hr, LANES), F32)],
    )(*scalars, *fields, *mats)


def block_shapes(part, planes, n, rows, ny):
    near = jax.ShapeDtypeStruct((planes, rows if part else rows // 2, ny), F32)
    return [near] * (n // 2) + far_shapes(planes, n, rows, ny)[: n // 2]


def own_body(device_ref, *refs):
    blocks, o_ref = refs[:-1], refs[-1]
    device = device_ref[0]
    n2 = len(blocks) // 3
    rows = blocks[0].shape[1]
    for k in range(n2):
        o_ref[0, pl.ds(pl.multiple_of((device ^ k) * rows, 8), rows), :] = blocks[k][0]
        at = pl.multiple_of((device ^ (n2 + k)) * rows, 8)
        o_ref[0, pl.ds(at, rows // 2), :] = blocks[n2 + k][0]
        o_ref[0, pl.ds(at + rows // 2, rows // 2), :] = blocks[2 * n2 + k][0]


def to_planes(blocks, device, nx):
    planes, _, ny = blocks[0].shape
    out = jax.ShapeDtypeStruct((planes, nx, ny), F32)
    return call(
        own_body,
        (planes,),
        [plane_spec(b) for b in blocks],
        plane_spec(out),
        out,
        moved=out.size * 8,
        prefetch=1,
    )(device, *blocks)


def local(densities, weights, spreads):
    _, planes, nx, ny = densities.shape
    n = lax.axis_size("sp")
    dens = lax.axis_size("dens")
    nz = planes * n
    n2 = n // 2
    rows = nx // n
    index = lax.axis_index("sp").astype(jnp.int32)
    device = jnp.stack([index, jnp.int32(n2)])
    by_core = dens == 2
    core = lax.axis_index("dens").astype(jnp.int32).reshape(1)
    here = core if by_core else jnp.zeros((1,), jnp.int32)
    swap = [(0, 1), (1, 0)]

    def xor_order(position, plane):
        return ((index ^ position) * planes + plane).astype(F32)

    natural = np.arange(nz)
    split_up = natural.reshape(n, 2, planes // 2).transpose(1, 0, 2).reshape(nz)
    halves = xor_order(split_up // planes, split_up % planes)
    blocks = xor_order(natural // planes, natural % planes)
    mats, (to_halves, to_blocks), inverses = all_weights(spreads, nx, ny, halves, blocks)

    if by_core:
        other_weight = lax.ppermute(weights[0], "dens", swap)
        total = weights[0] + other_weight
        alphas = jnp.stack([weights[0] / total, other_weight / total])
    else:
        own = weights[0] / lax.psum(weights[0], "dens")
        alphas = jnp.stack([own, jnp.ones_like(own)])

    def others(logs):
        if by_core:
            return lax.ppermute(logs, "dens", swap)
        return lax.psum(alphas[0] * logs, "dens") - alphas[0] * logs

    def trade(parts, first):
        return [
            part if first + k == 0 else lax.ppermute(part, "sp", [(i, i ^ (first + k)) for i in range(n)])
            for k, part in enumerate(parts)
        ]

    far = blur_part(densities[0], True, device, n, mats, inverses)
    near = blur_part(densities[0], False, device, n, mats, inverses)
    far = [trade(far[:n2], n2), trade(far[n2:], n2)]
    near = trade(near, 0)

    scale_v, sent = [], []
    line = jax.ShapeDtypeStruct((nz, rows // 2, ny), F32)
    for p in (0, 1):
        (logs,) = columns(
            functools.partial(log_body, n), p, (), (*near, *far[p]), (to_halves,), [line], nz, rows
        )
        rest = others(logs)
        before = sent[0][:n2] if p else []
        v, *out = columns(
            functools.partial(scale_body, p, n),
            p,
            (alphas,),
            (logs, rest, *before),
            (to_blocks,),
            [line, *block_shapes(p, planes, n, rows, ny)],
            nz,
            rows,
        )
        scale_v.append(v)
        sent.append(out)
    far = trade(sent[0][n2:], n2), trade(sent[1][n2:], n2)
    near = trade(sent[1][:n2], 0)

    scalings, far = blur_second([*near, *far[0], *far[1]], densities[0], device, n, mats)
    near = blur_part(scalings, False, device, n, mats)
    far = [trade(far[:n2], n2), trade(far[n2:], n2)]
    near = trade(near, 0)

    sent = []
    line = jax.ShapeDtypeStruct((nz // 2, rows // 2, ny), F32)
    hp = planes // 2
    for p in (0, 1):
        mine, send = columns(
            functools.partial(last_body, n),
            p,
            (here,),
            (scale_v[p], *near, *far[p]),
            (to_halves,),
            [line, line],
            nz,
            rows,
        )

        def exped(first, second, before):
            return columns(
                functools.partial(exp_body, p, n),
                p,
                (alphas,),
                (first, second, *before),
                (),
                block_shapes(p, hp, n, rows, ny),
                nz // 2,
                rows,
            )

        if by_core:
            send = lax.ppermute(send, "dens", swap)
            pairs = [(mine, send)]
        else:
            pairs = [(mine, others(mine)), (send, others(send))]
        sent.append(
            [exped(*pair, sent[0][q][:n2] if p else []) for q, pair in enumerate(pairs)]
        )
    parts = []
    for q in range(len(sent[0])):
        far = trade(sent[0][q][n2:], n2), trade(sent[1][q][n2:], n2)
        near = trade(sent[1][q][:n2], 0)
        parts.append(to_planes([*near, *far[0], *far[1]], device, nx))
    if by_core:
        other = lax.ppermute(parts[0], "dens", swap)
        first = jnp.where(core[0] == 0, parts[0], other)
        second = jnp.where(core[0] == 0, other, parts[0])
        parts = [first, second]
    return jnp.concatenate(parts, 0), scalings[None]


def solution(mesh):
    return jax.shard_map(
        local,
        mesh=mesh,
        in_specs=(P("dens", "sp", None, None), P("dens"), P()),
        out_specs=(P("sp", None, None), P("dens", "sp", None, None)),
        check_vma=False,
    )
```

```python
import functools

import jax
import jax.numpy as jnp
from jax import lax
from jax.experimental import pallas as pl
from jax.experimental.pallas import tpu as pltpu
from jax.sharding import PartitionSpec as P


LANES = 128
TILE = 256
REACH = 32
F32 = jnp.float32
BF16 = jnp.bfloat16


def gauss(diff, spread):
    scaled = diff / spread
    return jnp.exp(-scaled * scaled) / (spread * jnp.sqrt(jnp.float32(jnp.pi)))


def split(value):
    high = value.astype(BF16)
    return high, (value - high.astype(F32)).astype(BF16)


def dot(a, b):
    return jnp.dot(a, b, preferred_element_type=F32)


def call(body, grid, in_specs, out_specs, out_shape, flops=0, moved=0, prefetch=0, scratch=()):
    return pl.pallas_call(
        body,
        grid_spec=pltpu.PrefetchScalarGridSpec(
            num_scalar_prefetch=prefetch,
            grid=grid,
            in_specs=in_specs,
            out_specs=out_specs,
            scratch_shapes=scratch,
        ),
        out_shape=out_shape,
        compiler_params=pltpu.CompilerParams(vmem_limit_bytes=56 << 20),
        cost_estimate=pl.CostEstimate(flops=flops, bytes_accessed=moved, transcendentals=0),
    )


def whole(array):
    return pl.BlockSpec(array.shape, lambda *_: (0,) * array.ndim)


def windows(length, tile, margin):
    tile = min(tile, length)
    return [
        (t, t + tile, max(t - margin, 0), min(t + tile + margin, length))
        for t in range(0, length, tile)
    ]


def row_windows(nx):
    return windows(nx, nx // 2, REACH)


def lane_windows(ny):
    return windows(ny, TILE, LANES)


def count(shape, dim, first=0):
    return (lax.broadcasted_iota(jnp.int32, shape, dim) + first).astype(F32)


def weights_body(nx, ny, planes, device_ref, spread_ref, *refs):
    refs = list(refs)
    rows_ref = refs.pop(0)
    for t, (start, stop, low, high) in enumerate(row_windows(nx)):
        shape = (stop - start, high - low)
        top, rest = split(gauss(count(shape, 0, start) - count(shape, 1, low), spread_ref[1]))
        rows_ref[t] = jnp.concatenate([top, top, rest], 1)
    for start, stop, low, high in lane_windows(ny):
        shape = (high - low, stop - start)
        top, rest = split(gauss(count(shape, 0, low) - count(shape, 1, start), spread_ref[2]))
        refs.pop(0)[...] = jnp.concatenate([top, top, rest], 0)
    halves_ref, blocks_ref, z_ref, x_ref, y_ref = refs
    nz = z_ref.shape[1]
    shape = (nz, nz)
    spread = spread_ref[0]

    def blocks(dim):
        at = lax.broadcasted_iota(jnp.int32, shape, dim)
        return (((device_ref[0] ^ (at // planes)) * planes) + at % planes).astype(F32)

    def halves(dim):
        at = lax.broadcasted_iota(jnp.int32, shape, dim)
        part = planes // 2
        rest = at % (nz // 2)
        plane = (device_ref[0] ^ (rest // part)) * planes + at // (nz // 2) * part
        return (plane + rest % part).astype(F32)

    for ref, diff in (
        (halves_ref, halves(0) - blocks(1)),
        (blocks_ref, blocks(0) - halves(1)),
    ):
        top, rest = split(gauss(diff, spread))
        ref[...] = jnp.concatenate([top, top, rest], 1)
    z_ref[...] = 1.0 / jnp.sum(
        gauss(count(shape, 0) - count(shape, 1), spread), axis=0, keepdims=True
    )
    for ref, axis, length, k in ((x_ref, 1, nx, 1), (y_ref, 0, ny, 2)):
        diff = count((length, length), 0) - count((length, length), 1)
        ref[...] = 1.0 / jnp.sum(gauss(diff, spread_ref[k]), axis=axis, keepdims=True)


def all_weights(spreads, device, nx, ny, nz, planes):
    start, stop, low, high = row_windows(nx)[0]
    shapes = [((2, stop - start, 3 * (high - low)), BF16)]
    shapes += [((3 * (h - l), e - s), BF16) for s, e, l, h in lane_windows(ny)]
    shapes += [((nz, 3 * nz), BF16)] * 2 + [((1, nz), F32), ((nx, 1), F32), ((1, ny), F32)]
    out = [jax.ShapeDtypeStruct(*s) for s in shapes]
    got = call(
        functools.partial(weights_body, nx, ny, planes),
        (1,),
        [],
        [whole(s) for s in out],
        out,
        prefetch=2,
    )(device, spreads)
    return got[:-5], got[-5:-3], got[-3:]


def blur_lanes(field, lane_refs):
    hi, lo = split(field)
    tiles = []
    for (_, _, low, high), lane_ref in zip(lane_windows(field.shape[1]), lane_refs):
        lhs = jnp.concatenate([hi[:, low:high], lo[:, low:high], hi[:, low:high]], 1)
        tiles.append(dot(lhs, lane_ref[...]))
    return split(jnp.concatenate(tiles, 1))


def blur_rows(parts, row_mat):
    hi, lo = parts
    return dot(row_mat, jnp.concatenate([hi, lo, hi], 0))


def row_start(nx, tile):
    return pl.multiple_of(tile * row_windows(nx)[1][2], 8)


def row_size(nx):
    return row_windows(nx)[0][3]


def give_blocks(device, far, tile_ref, refs):
    n2 = len(refs) // 2 if far else len(refs)
    for k in range(n2):
        rows = refs[k].shape[1] * (2 if far else 1)
        at = pl.multiple_of(((device ^ k) & (n2 - 1)) * rows, 8)
        if far:
            refs[k][0] = tile_ref[pl.ds(at, rows // 2), :]
            refs[n2 + k][0] = tile_ref[pl.ds(at + rows // 2, rows // 2), :]
        else:
            refs[k][0] = tile_ref[pl.ds(at, rows), :]


def tile_body(far, n2, scaled, n_lanes, device_ref, f_ref, *refs):
    _, nx, _ = f_ref.shape
    refs = list(refs)
    device = device_ref[0]
    half = device // n2
    tile = 1 - half if far else half
    window = pl.ds(row_start(nx, tile), row_size(nx))
    field = f_ref[0, window, :]
    if scaled:
        z_ref, x_ref, y_ref = refs[:3]
        refs = refs[3:]
        plane = device * pl.num_programs(0) + pl.program_id(0)
        at = lax.broadcasted_iota(jnp.int32, z_ref.shape, 1) == plane
        scale = jnp.sum(jnp.where(at, z_ref[...], 0.0), axis=1, keepdims=True)
        field = field * x_ref[window, :] * (y_ref[...] * scale)
    rows_ref, lane_refs, outs, tile_ref = refs[0], refs[1 : 1 + n_lanes], refs[1 + n_lanes : -1], refs[-1]

    tile_ref[...] = blur_rows(blur_lanes(field, lane_refs), rows_ref[tile])
    give_blocks(device, far, tile_ref, outs)


def second_body(n_in, n_lanes, device_ref, t_ref, *refs):
    _, nx, _ = t_ref.shape
    blocks, refs = refs[:n_in], refs[n_in:]
    rows_ref, lane_refs, refs = refs[0], refs[1 : 1 + n_lanes], refs[1 + n_lanes :]
    w_ref, outs, field_ref, tile_ref = refs[0], refs[1:-2], refs[-2], refs[-1]
    device = device_ref[0]
    n2 = n_in // 3
    rows = blocks[0].shape[1]
    for k in range(n2):
        field_ref[pl.ds(pl.multiple_of((device ^ k) * rows, 8), rows), :] = blocks[k][0]
        at = pl.multiple_of((device ^ (n2 + k)) * rows, 8)
        field_ref[pl.ds(at, rows // 2), :] = blocks[n2 + k][0]
        field_ref[pl.ds(at + rows // 2, rows // 2), :] = blocks[2 * n2 + k][0]
    hi, lo = blur_lanes(field_ref[...], lane_refs)
    for t, (start, stop, low, high) in enumerate(row_windows(nx)):
        blurred = blur_rows((hi[low:high], lo[low:high]), rows_ref[t])
        w_ref[0, start:stop, :] = t_ref[0, start:stop, :] / blurred
    tile = 1 - device // n2
    field = w_ref[0, pl.ds(row_start(nx, tile), row_size(nx)), :]
    tile_ref[...] = blur_rows(blur_lanes(field, lane_refs), rows_ref[tile])
    give_blocks(device, True, tile_ref, outs)


def plane_spec(field):
    return pl.BlockSpec((1,) + field.shape[1:], lambda k, *_: (k, 0, 0))


def far_shapes(planes, n, rows, ny):
    return [jax.ShapeDtypeStruct((planes, rows // 2, ny), F32)] * n


def near_shapes(planes, n, rows, ny):
    return [jax.ShapeDtypeStruct((planes, rows, ny), F32)] * (n // 2)


def blur_part(field, far, device, n, mats, inverses=()):
    planes, nx, ny = field.shape
    out = (far_shapes if far else near_shapes)(planes, n, nx // n, ny)
    return call(
        functools.partial(tile_body, far, n // 2, bool(inverses), len(mats) - 1),
        (planes,),
        [plane_spec(field), *map(whole, inverses), *map(whole, mats)],
        [plane_spec(o) for o in out],
        out,
        flops=6 * field.size * TILE,
        moved=6 * field.size,
        prefetch=1,
        scratch=[pltpu.VMEM((nx // 2, ny), F32)],
    )(device, field, *inverses, *mats)


def blur_second(blocks, target, device, n, mats):
    planes, nx, ny = target.shape
    out = [jax.ShapeDtypeStruct(target.shape, F32), *far_shapes(planes, n, nx // n, ny)]
    w, *far = call(
        functools.partial(second_body, len(blocks), len(mats) - 1),
        (planes,),
        [plane_spec(target), *map(plane_spec, blocks), *map(whole, mats)],
        [plane_spec(o) for o in out],
        out,
        flops=18 * target.size * TILE,
        moved=14 * target.size,
        prefetch=1,
        scratch=[pltpu.VMEM((nx, ny), F32), pltpu.VMEM((nx // 2, ny), F32)],
    )(device, target, *blocks, *mats)
    return w, far


def z_blur(m_ref, column_of, store, rows):
    for x in range(0, rows, 2):
        cols = []
        for k in (x, x + 1):
            hi, lo = split(column_of(k))
            cols.append(jnp.concatenate([hi, lo, hi], 0))
        both = dot(m_ref[...], jnp.concatenate(cols, 1))
        store(x, both[:, :LANES])
        store(x + 1, both[:, LANES:])


def rows_of(ref, x):
    planes, bx, _ = ref.shape
    return ref.reshape(planes * bx, LANES)[pl.ds(x, planes, stride=bx), :]


def put_rows(ref, x, value):
    planes, bx, _ = ref.shape
    ref.reshape(planes * bx, LANES)[pl.ds(x, planes, stride=bx), :] = value


def gather(blocks, field_ref):
    planes = blocks[0].shape[0]
    for k, block in enumerate(blocks):
        field_ref[k * planes : (k + 1) * planes] = block[...]


def spread_out(field_ref, part, befores, refs):
    n2 = len(refs) // 2
    planes, hr, _ = refs[-1].shape
    for k, ref in enumerate(refs):
        value = field_ref[k * planes : (k + 1) * planes]
        if k < n2 and part == 1:
            ref[:, :hr] = befores[k][...]
            ref[:, hr:] = value
        else:
            ref[...] = value


def log_body(n, *refs):
    blocks, m_ref, l_ref, field_ref = refs[:n], refs[n], refs[n + 1], refs[n + 2]
    gather(blocks, field_ref)

    def store(x, value):
        put_rows(l_ref, x, jnp.log(value))

    z_blur(m_ref, lambda x: rows_of(field_ref, x), store, l_ref.shape[1])


def scale_body(part, n, alpha_ref, l_ref, o_ref, *refs):
    n_before = n // 2 if part else 0
    befores, m_ref, v_ref = refs[:n_before], refs[n_before], refs[n_before + 1]
    outs, field_ref = refs[n_before + 2 : -1], refs[-1]
    logs = l_ref[...]
    v_ref[...] = jnp.exp(alpha_ref[0] * logs + alpha_ref[1] * o_ref[...] - logs)

    def store(x, value):
        put_rows(field_ref, x, value)

    z_blur(m_ref, lambda x: rows_of(v_ref, x), store, l_ref.shape[1])
    spread_out(field_ref, part, befores, outs)


def last_body(n, core_ref, v_ref, *refs):
    blocks, m_ref, mine_ref, send_ref, field_ref = refs[:n], *refs[n:]
    nz, hr, _ = v_ref.shape
    gather(blocks, field_ref)

    def run(out):
        def store(x, value):
            value = jnp.log(rows_of(v_ref, x) * value)
            put_rows(out[0], x, value[: nz // 2])
            put_rows(out[1], x, value[nz // 2 :])

        z_blur(m_ref, lambda x: rows_of(field_ref, x), store, hr)

    @pl.when(core_ref[0] == 0)
    def _():
        run((mine_ref, send_ref))

    @pl.when(core_ref[0] != 0)
    def _():
        run((send_ref, mine_ref))


def exp_body(part, n, alpha_ref, mine_ref, other_ref, *refs):
    n_before = n // 2 if part else 0
    befores, outs, field_ref = refs[:n_before], refs[n_before:-1], refs[-1]
    field_ref[...] = jnp.exp(alpha_ref[0] * mine_ref[...] + alpha_ref[1] * other_ref[...])
    spread_out(field_ref, part, befores, outs)


def columns(body, part, scalars, fields, mats, out_shape, scratch_planes, rows, lanes=LANES):
    hr = rows // 2

    def spec(s):
        if s.shape[1] == hr:
            return pl.BlockSpec((s.shape[0], hr, lanes), lambda i, *_: (0, 0, i))
        return pl.BlockSpec((s.shape[0], hr, lanes), lambda i, *_: (0, part, i))

    def out_spec(s):
        return pl.BlockSpec((s.shape[0], s.shape[1], lanes), lambda i, *_: (0, 0, i))

    ny = fields[0].shape[2]
    planes = sum(f.shape[0] for f in fields) + sum(s.shape[0] for s in out_shape)
    return call(
        body,
        (ny // lanes,),
        [*map(spec, fields), *map(whole, mats)],
        [out_spec(s) for s in out_shape],
        out_shape,
        flops=12 * scratch_planes * scratch_planes * hr * ny,
        moved=planes * hr * ny * 4,
        prefetch=len(scalars),
        scratch=[pltpu.VMEM((scratch_planes, hr, lanes), F32)],
    )(*scalars, *fields, *mats)


def block_shapes(part, planes, n, rows, ny):
    near = jax.ShapeDtypeStruct((planes, rows if part else rows // 2, ny), F32)
    return [near] * (n // 2) + far_shapes(planes, n, rows, ny)[: n // 2]


def own_body(device_ref, *refs):
    blocks, o_ref = refs[:-1], refs[-1]
    device = device_ref[0]
    n2 = len(blocks) // 3
    rows = blocks[0].shape[1]
    for k in range(n2):
        o_ref[0, pl.ds(pl.multiple_of((device ^ k) * rows, 8), rows), :] = blocks[k][0]
        at = pl.multiple_of((device ^ (n2 + k)) * rows, 8)
        o_ref[0, pl.ds(at, rows // 2), :] = blocks[n2 + k][0]
        o_ref[0, pl.ds(at + rows // 2, rows // 2), :] = blocks[2 * n2 + k][0]


def to_planes(blocks, device, nx):
    planes, _, ny = blocks[0].shape
    out = jax.ShapeDtypeStruct((planes, nx, ny), F32)
    return call(
        own_body,
        (planes,),
        [plane_spec(b) for b in blocks],
        plane_spec(out),
        out,
        moved=out.size * 8,
        prefetch=1,
    )(device, *blocks)


def local(densities, weights, spreads):
    _, planes, nx, ny = densities.shape
    n = lax.axis_size("sp")
    dens = lax.axis_size("dens")
    nz = planes * n
    n2 = n // 2
    rows = nx // n
    device = lax.axis_index("sp").astype(jnp.int32).reshape(1)
    by_core = dens == 2
    core = lax.axis_index("dens").astype(jnp.int32).reshape(1)
    here = core if by_core else jnp.zeros((1,), jnp.int32)
    swap = [(0, 1), (1, 0)]

    mats, (to_halves, to_blocks), inverses = all_weights(spreads, device, nx, ny, nz, planes)

    if by_core:
        other_weight = lax.ppermute(weights[0], "dens", swap)
        total = weights[0] + other_weight
        alphas = jnp.stack([weights[0] / total, other_weight / total])
    else:
        own = weights[0] / lax.psum(weights[0], "dens")
        alphas = jnp.stack([own, jnp.ones_like(own)])

    def others(logs):
        if by_core:
            return lax.ppermute(logs, "dens", swap)
        return lax.psum(alphas[0] * logs, "dens") - alphas[0] * logs

    def trade(parts, first):
        return [
            part if first + k == 0 else lax.ppermute(part, "sp", [(i, i ^ (first + k)) for i in range(n)])
            for k, part in enumerate(parts)
        ]

    far = blur_part(densities[0], True, device, n, mats, inverses)
    near = blur_part(densities[0], False, device, n, mats, inverses)
    far = [trade(far[:n2], n2), trade(far[n2:], n2)]
    near = trade(near, 0)

    scale_v, sent = [], []
    line = jax.ShapeDtypeStruct((nz, rows // 2, ny), F32)
    for p in (0, 1):
        (logs,) = columns(
            functools.partial(log_body, n), p, (), (*near, *far[p]), (to_halves,), [line], nz, rows
        )
        rest = others(logs)
        before = sent[0][:n2] if p else []
        v, *out = columns(
            functools.partial(scale_body, p, n),
            p,
            (alphas,),
            (logs, rest, *before),
            (to_blocks,),
            [line, *block_shapes(p, planes, n, rows, ny)],
            nz,
            rows,
        )
        scale_v.append(v)
        sent.append(out)
    far = trade(sent[0][n2:], n2), trade(sent[1][n2:], n2)
    near = trade(sent[1][:n2], 0)

    scalings, far = blur_second([*near, *far[0], *far[1]], densities[0], device, n, mats)
    near = blur_part(scalings, False, device, n, mats)
    far = [trade(far[:n2], n2), trade(far[n2:], n2)]
    near = trade(near, 0)

    sent = []
    line = jax.ShapeDtypeStruct((nz // 2, rows // 2, ny), F32)
    hp = planes // 2
    for p in (0, 1):
        mine, send = columns(
            functools.partial(last_body, n),
            p,
            (here,),
            (scale_v[p], *near, *far[p]),
            (to_halves,),
            [line, line],
            nz,
            rows,
        )

        def exped(first, second, before):
            return columns(
                functools.partial(exp_body, p, n),
                p,
                (alphas,),
                (first, second, *before),
                (),
                block_shapes(p, hp, n, rows, ny),
                nz // 2,
                rows,
                2 * LANES,
            )

        if by_core:
            send = lax.ppermute(send, "dens", swap)
            pairs = [(mine, send)]
        else:
            pairs = [(mine, others(mine)), (send, others(send))]
        sent.append(
            [exped(*pair, sent[0][q][:n2] if p else []) for q, pair in enumerate(pairs)]
        )
    parts = []
    for q in range(len(sent[0])):
        far = trade(sent[0][q][n2:], n2), trade(sent[1][q][n2:], n2)
        near = trade(sent[1][q][:n2], 0)
        parts.append(to_planes([*near, *far[0], *far[1]], device, nx))
    if by_core:
        other = lax.ppermute(parts[0], "dens", swap)
        mine = jnp.arange(2)[:, None, None, None] == core[0]
        bary = jnp.where(mine, parts[0][None], other[None])
        return bary.reshape(planes, nx, ny), scalings[None]
    return jnp.concatenate(parts, 0), scalings[None]


def solution(mesh):
    return jax.shard_map(
        local,
        mesh=mesh,
        in_specs=(P("dens", "sp", None, None), P("dens"), P()),
        out_specs=(P("sp", None, None), P("dens", "sp", None, None)),
        check_vma=False,
    )
```

```python
import functools

import jax
import jax.numpy as jnp
from jax import lax
from jax.experimental import pallas as pl
from jax.experimental.pallas import tpu as pltpu
from jax.sharding import PartitionSpec as P


LANES = 128
TILE = 256
REACH = 32
F32 = jnp.float32
BF16 = jnp.bfloat16


def gauss(diff, spread):
    scaled = diff / spread
    return jnp.exp(-scaled * scaled) / (spread * jnp.sqrt(jnp.float32(jnp.pi)))


def split(value):
    high = value.astype(BF16)
    return high, (value - high.astype(F32)).astype(BF16)


def dot(a, b):
    return jnp.dot(a, b, preferred_element_type=F32)


def call(body, grid, in_specs, out_specs, out_shape, flops=0, moved=0, prefetch=0, scratch=()):
    return pl.pallas_call(
        body,
        grid_spec=pltpu.PrefetchScalarGridSpec(
            num_scalar_prefetch=prefetch,
            grid=grid,
            in_specs=in_specs,
            out_specs=out_specs,
            scratch_shapes=scratch,
        ),
        out_shape=out_shape,
        compiler_params=pltpu.CompilerParams(vmem_limit_bytes=56 << 20),
        cost_estimate=pl.CostEstimate(flops=flops, bytes_accessed=moved, transcendentals=0),
    )


def whole(array):
    return pl.BlockSpec(array.shape, lambda *_: (0,) * array.ndim)


def windows(length, tile, margin):
    tile = min(tile, length)
    return [
        (t, t + tile, max(t - margin, 0), min(t + tile + margin, length))
        for t in range(0, length, tile)
    ]


def row_windows(nx):
    return windows(nx, nx // 2, REACH)


def lane_windows(ny):
    return windows(ny, TILE, LANES)


def count(shape, dim, first=0):
    return (lax.broadcasted_iota(jnp.int32, shape, dim) + first).astype(F32)


def weights_body(nx, ny, planes, device_ref, spread_ref, *refs):
    refs = list(refs)
    rows_ref = refs.pop(0)
    for t, (start, stop, low, high) in enumerate(row_windows(nx)):
        shape = (stop - start, high - low)
        top, rest = split(gauss(count(shape, 0, start) - count(shape, 1, low), spread_ref[1]))
        rows_ref[t] = jnp.concatenate([top, top, rest], 1)
    for start, stop, low, high in lane_windows(ny):
        shape = (high - low, stop - start)
        top, rest = split(gauss(count(shape, 0, low) - count(shape, 1, start), spread_ref[2]))
        refs.pop(0)[...] = jnp.concatenate([top, top, rest], 0)
    halves_ref, blocks_ref, z_ref, x_ref, y_ref = refs
    nz = z_ref.shape[1]
    shape = (nz, nz)
    spread = spread_ref[0]

    def blocks(dim):
        at = lax.broadcasted_iota(jnp.int32, shape, dim)
        return (((device_ref[0] ^ (at // planes)) * planes) + at % planes).astype(F32)

    def halves(dim):
        at = lax.broadcasted_iota(jnp.int32, shape, dim)
        part = planes // 2
        rest = at % (nz // 2)
        plane = (device_ref[0] ^ (rest // part)) * planes + at // (nz // 2) * part
        return (plane + rest % part).astype(F32)

    for ref, diff in (
        (halves_ref, halves(0) - blocks(1)),
        (blocks_ref, blocks(0) - halves(1)),
    ):
        top, rest = split(gauss(diff, spread))
        ref[...] = jnp.concatenate([top, top, rest], 1)
    z_ref[...] = 1.0 / jnp.sum(
        gauss(count(shape, 0) - count(shape, 1), spread), axis=0, keepdims=True
    )
    for ref, axis, length, k in ((x_ref, 1, nx, 1), (y_ref, 0, ny, 2)):
        diff = count((length, length), 0) - count((length, length), 1)
        ref[...] = 1.0 / jnp.sum(gauss(diff, spread_ref[k]), axis=axis, keepdims=True)


def all_weights(spreads, device, nx, ny, nz, planes):
    start, stop, low, high = row_windows(nx)[0]
    shapes = [((2, stop - start, 3 * (high - low)), BF16)]
    shapes += [((3 * (h - l), e - s), BF16) for s, e, l, h in lane_windows(ny)]
    shapes += [((nz, 3 * nz), BF16)] * 2 + [((1, nz), F32), ((nx, 1), F32), ((1, ny), F32)]
    out = [jax.ShapeDtypeStruct(*s) for s in shapes]
    got = call(
        functools.partial(weights_body, nx, ny, planes),
        (1,),
        [],
        [whole(s) for s in out],
        out,
        prefetch=2,
    )(device, spreads)
    return got[:-5], got[-5:-3], got[-3:]


def blur_lanes(field, lane_refs):
    hi, lo = split(field)
    tiles = []
    for (_, _, low, high), lane_ref in zip(lane_windows(field.shape[1]), lane_refs):
        lhs = jnp.concatenate([hi[:, low:high], lo[:, low:high], hi[:, low:high]], 1)
        tiles.append(dot(lhs, lane_ref[...]))
    return split(jnp.concatenate(tiles, 1))


def blur_rows(parts, row_mat):
    hi, lo = parts
    return dot(row_mat, jnp.concatenate([hi, lo, hi], 0))


def row_start(nx, tile):
    return pl.multiple_of(tile * row_windows(nx)[1][2], 8)


def row_size(nx):
    return row_windows(nx)[0][3]


def give_blocks(device, far, tile_ref, refs):
    n2 = len(refs) // 2 if far else len(refs)
    for k in range(n2):
        rows = refs[k].shape[1] * (2 if far else 1)
        at = pl.multiple_of(((device ^ k) & (n2 - 1)) * rows, 8)
        if far:
            refs[k][0] = tile_ref[pl.ds(at, rows // 2), :]
            refs[n2 + k][0] = tile_ref[pl.ds(at + rows // 2, rows // 2), :]
        else:
            refs[k][0] = tile_ref[pl.ds(at, rows), :]


def tile_body(far, n2, scaled, n_lanes, device_ref, f_ref, *refs):
    _, nx, _ = f_ref.shape
    refs = list(refs)
    device = device_ref[0]
    half = device // n2
    tile = 1 - half if far else half
    window = pl.ds(row_start(nx, tile), row_size(nx))
    field = f_ref[0, window, :]
    if scaled:
        z_ref, x_ref, y_ref = refs[:3]
        refs = refs[3:]
        plane = device * pl.num_programs(0) + pl.program_id(0)
        at = lax.broadcasted_iota(jnp.int32, z_ref.shape, 1) == plane
        scale = jnp.sum(jnp.where(at, z_ref[...], 0.0), axis=1, keepdims=True)
        field = field * x_ref[window, :] * (y_ref[...] * scale)
    rows_ref, lane_refs, outs, tile_ref = refs[0], refs[1 : 1 + n_lanes], refs[1 + n_lanes : -1], refs[-1]

    tile_ref[...] = blur_rows(blur_lanes(field, lane_refs), rows_ref[tile])
    give_blocks(device, far, tile_ref, outs)


def second_body(n_in, n_lanes, device_ref, t_ref, *refs):
    _, nx, _ = t_ref.shape
    blocks, refs = refs[:n_in], refs[n_in:]
    rows_ref, lane_refs, refs = refs[0], refs[1 : 1 + n_lanes], refs[1 + n_lanes :]
    w_ref, outs, field_ref, tile_ref = refs[0], refs[1:-2], refs[-2], refs[-1]
    device = device_ref[0]
    n2 = n_in // 3
    rows = blocks[0].shape[1]
    for k in range(n2):
        field_ref[pl.ds(pl.multiple_of((device ^ k) * rows, 8), rows), :] = blocks[k][0]
        at = pl.multiple_of((device ^ (n2 + k)) * rows, 8)
        field_ref[pl.ds(at, rows // 2), :] = blocks[n2 + k][0]
        field_ref[pl.ds(at + rows // 2, rows // 2), :] = blocks[2 * n2 + k][0]
    hi, lo = blur_lanes(field_ref[...], lane_refs)
    for t, (start, stop, low, high) in enumerate(row_windows(nx)):
        blurred = blur_rows((hi[low:high], lo[low:high]), rows_ref[t])
        w_ref[0, start:stop, :] = t_ref[0, start:stop, :] / blurred
    tile = 1 - device // n2
    field = w_ref[0, pl.ds(row_start(nx, tile), row_size(nx)), :]
    tile_ref[...] = blur_rows(blur_lanes(field, lane_refs), rows_ref[tile])
    give_blocks(device, True, tile_ref, outs)


def plane_spec(field):
    return pl.BlockSpec((1,) + field.shape[1:], lambda k, *_: (k, 0, 0))


def far_shapes(planes, n, rows, ny):
    return [jax.ShapeDtypeStruct((planes, rows // 2, ny), F32)] * n


def near_shapes(planes, n, rows, ny):
    return [jax.ShapeDtypeStruct((planes, rows, ny), F32)] * (n // 2)


def blur_part(field, far, device, n, mats, inverses=()):
    planes, nx, ny = field.shape
    out = (far_shapes if far else near_shapes)(planes, n, nx // n, ny)
    return call(
        functools.partial(tile_body, far, n // 2, bool(inverses), len(mats) - 1),
        (planes,),
        [plane_spec(field), *map(whole, inverses), *map(whole, mats)],
        [plane_spec(o) for o in out],
        out,
        flops=6 * field.size * TILE,
        moved=6 * field.size,
        prefetch=1,
        scratch=[pltpu.VMEM((nx // 2, ny), F32)],
    )(device, field, *inverses, *mats)


def blur_second(blocks, target, device, n, mats):
    planes, nx, ny = target.shape
    out = [jax.ShapeDtypeStruct(target.shape, F32), *far_shapes(planes, n, nx // n, ny)]
    w, *far = call(
        functools.partial(second_body, len(blocks), len(mats) - 1),
        (planes,),
        [plane_spec(target), *map(plane_spec, blocks), *map(whole, mats)],
        [plane_spec(o) for o in out],
        out,
        flops=18 * target.size * TILE,
        moved=14 * target.size,
        prefetch=1,
        scratch=[pltpu.VMEM((nx, ny), F32), pltpu.VMEM((nx // 2, ny), F32)],
    )(device, target, *blocks, *mats)
    return w, far


def z_blur(m_ref, column_of, store, rows):
    for x in range(0, rows, 2):
        cols = []
        for k in (x, x + 1):
            hi, lo = split(column_of(k))
            cols.append(jnp.concatenate([hi, lo, hi], 0))
        both = dot(m_ref[...], jnp.concatenate(cols, 1))
        store(x, both[:, :LANES])
        store(x + 1, both[:, LANES:])


def rows_of(ref, x):
    planes, bx, _ = ref.shape
    return ref.reshape(planes * bx, LANES)[pl.ds(x, planes, stride=bx), :]


def put_rows(ref, x, value):
    planes, bx, _ = ref.shape
    ref.reshape(planes * bx, LANES)[pl.ds(x, planes, stride=bx), :] = value


def gather(blocks, field_ref):
    planes = blocks[0].shape[0]
    for k, block in enumerate(blocks):
        field_ref[k * planes : (k + 1) * planes] = block[...]


def spread_out(field_ref, part, befores, refs):
    n2 = len(refs) // 2
    planes, hr, _ = refs[-1].shape
    for k, ref in enumerate(refs):
        value = field_ref[k * planes : (k + 1) * planes]
        if k < n2 and part == 1:
            ref[:, :hr] = befores[k][...]
            ref[:, hr:] = value
        else:
            ref[...] = value


def log_body(n, *refs):
    blocks, m_ref, l_ref, field_ref = refs[:n], refs[n], refs[n + 1], refs[n + 2]
    gather(blocks, field_ref)

    def store(x, value):
        put_rows(l_ref, x, jnp.log(value))

    z_blur(m_ref, lambda x: rows_of(field_ref, x), store, l_ref.shape[1])


def scale_body(part, n, alpha_ref, l_ref, o_ref, *refs):
    n_before = n // 2 if part else 0
    befores, m_ref, v_ref = refs[:n_before], refs[n_before], refs[n_before + 1]
    outs, field_ref = refs[n_before + 2 : -1], refs[-1]
    logs = l_ref[...]
    v_ref[...] = jnp.exp(alpha_ref[0] * logs + alpha_ref[1] * o_ref[...] - logs)

    def store(x, value):
        put_rows(field_ref, x, value)

    z_blur(m_ref, lambda x: rows_of(v_ref, x), store, l_ref.shape[1])
    spread_out(field_ref, part, befores, outs)


def last_body(n, core_ref, v_ref, *refs):
    blocks, m_ref, mine_ref, send_ref, field_ref = refs[:n], *refs[n:]
    nz, hr, _ = v_ref.shape
    gather(blocks, field_ref)

    def run(out):
        def store(x, value):
            value = jnp.log(rows_of(v_ref, x) * value)
            put_rows(out[0], x, value[: nz // 2])
            put_rows(out[1], x, value[nz // 2 :])

        z_blur(m_ref, lambda x: rows_of(field_ref, x), store, hr)

    @pl.when(core_ref[0] == 0)
    def _():
        run((mine_ref, send_ref))

    @pl.when(core_ref[0] != 0)
    def _():
        run((send_ref, mine_ref))


def exp_body(part, n, alpha_ref, mine_ref, other_ref, *refs):
    n_before = n // 2 if part else 0
    befores, outs, field_ref = refs[:n_before], refs[n_before:-1], refs[-1]
    field_ref[...] = jnp.exp(alpha_ref[0] * mine_ref[...] + alpha_ref[1] * other_ref[...])
    spread_out(field_ref, part, befores, outs)


def columns(body, part, scalars, fields, mats, out_shape, scratch_planes, rows, lanes=LANES):
    hr = rows // 2

    def spec(s):
        if s.shape[1] == hr:
            return pl.BlockSpec((s.shape[0], hr, lanes), lambda i, *_: (0, 0, i))
        return pl.BlockSpec((s.shape[0], hr, lanes), lambda i, *_: (0, part, i))

    def out_spec(s):
        return pl.BlockSpec((s.shape[0], s.shape[1], lanes), lambda i, *_: (0, 0, i))

    ny = fields[0].shape[2]
    planes = sum(f.shape[0] for f in fields) + sum(s.shape[0] for s in out_shape)
    return call(
        body,
        (ny // lanes,),
        [*map(spec, fields), *map(whole, mats)],
        [out_spec(s) for s in out_shape],
        out_shape,
        flops=12 * scratch_planes * scratch_planes * hr * ny,
        moved=planes * hr * ny * 4,
        prefetch=len(scalars),
        scratch=[pltpu.VMEM((scratch_planes, hr, lanes), F32)],
    )(*scalars, *fields, *mats)


def block_shapes(part, planes, n, rows, ny):
    near = jax.ShapeDtypeStruct((planes, rows if part else rows // 2, ny), F32)
    return [near] * (n // 2) + far_shapes(planes, n, rows, ny)[: n // 2]


def own_body(device_ref, *refs):
    blocks, o_ref = refs[:-1], refs[-1]
    device = device_ref[0]
    n2 = len(blocks) // 3
    rows = blocks[0].shape[1]
    for k in range(n2):
        o_ref[0, pl.ds(pl.multiple_of((device ^ k) * rows, 8), rows), :] = blocks[k][0]
        at = pl.multiple_of((device ^ (n2 + k)) * rows, 8)
        o_ref[0, pl.ds(at, rows // 2), :] = blocks[n2 + k][0]
        o_ref[0, pl.ds(at + rows // 2, rows // 2), :] = blocks[2 * n2 + k][0]


def to_planes(blocks, device, nx):
    planes, _, ny = blocks[0].shape
    out = jax.ShapeDtypeStruct((planes, nx, ny), F32)
    return call(
        own_body,
        (planes,),
        [plane_spec(b) for b in blocks],
        plane_spec(out),
        out,
        moved=out.size * 8,
        prefetch=1,
    )(device, *blocks)


def local(densities, weights, spreads):
    _, planes, nx, ny = densities.shape
    n = lax.axis_size("sp")
    dens = lax.axis_size("dens")
    nz = planes * n
    n2 = n // 2
    rows = nx // n
    device = lax.axis_index("sp").astype(jnp.int32).reshape(1)
    by_core = dens == 2
    core = lax.axis_index("dens").astype(jnp.int32).reshape(1)
    here = core if by_core else jnp.zeros((1,), jnp.int32)
    swap = [(0, 1), (1, 0)]

    mats, (to_halves, to_blocks), inverses = all_weights(spreads, device, nx, ny, nz, planes)

    if by_core:
        other_weight = lax.ppermute(weights[0], "dens", swap)
        total = weights[0] + other_weight
        alphas = jnp.stack([weights[0] / total, other_weight / total])
    else:
        own = weights[0] / lax.psum(weights[0], "dens")
        alphas = jnp.stack([own, jnp.ones_like(own)])

    def others(logs):
        if by_core:
            return lax.ppermute(logs, "dens", swap)
        return lax.psum(alphas[0] * logs, "dens") - alphas[0] * logs

    def trade(parts, first):
        moved = []
        for k, part in enumerate(parts, first):
            pairs = [(i, i ^ k) for i in range(n)]
            moved.append(lax.ppermute(part, "sp", pairs) if k else part)
        return moved

    far = blur_part(densities[0], True, device, n, mats, inverses)
    near = blur_part(densities[0], False, device, n, mats, inverses)
    far = [trade(far[:n2], n2), trade(far[n2:], n2)]
    near = trade(near, 0)

    scale_v, sent = [], []
    line = jax.ShapeDtypeStruct((nz, rows // 2, ny), F32)
    for p in (0, 1):
        (logs,) = columns(
            functools.partial(log_body, n), p, (), (*near, *far[p]), (to_halves,), [line], nz, rows
        )
        rest = others(logs)
        before = sent[0][:n2] if p else []
        v, *out = columns(
            functools.partial(scale_body, p, n),
            p,
            (alphas,),
            (logs, rest, *before),
            (to_blocks,),
            [line, *block_shapes(p, planes, n, rows, ny)],
            nz,
            rows,
        )
        scale_v.append(v)
        sent.append(out)
    far = trade(sent[0][n2:], n2), trade(sent[1][n2:], n2)
    near = trade(sent[1][:n2], 0)

    scalings, far = blur_second([*near, *far[0], *far[1]], densities[0], device, n, mats)
    near = blur_part(scalings, False, device, n, mats)
    far = [trade(far[:n2], n2), trade(far[n2:], n2)]
    near = trade(near, 0)

    sent = []
    line = jax.ShapeDtypeStruct((nz // 2, rows // 2, ny), F32)
    hp = planes // 2
    for p in (0, 1):
        mine, send = columns(
            functools.partial(last_body, n),
            p,
            (here,),
            (scale_v[p], *near, *far[p]),
            (to_halves,),
            [line, line],
            nz,
            rows,
        )

        def exped(first, second, before):
            return columns(
                functools.partial(exp_body, p, n),
                p,
                (alphas,),
                (first, second, *before),
                (),
                block_shapes(p, hp, n, rows, ny),
                nz // 2,
                rows,
                2 * LANES,
            )

        if by_core:
            send = lax.ppermute(send, "dens", swap)
            pairs = [(mine, send)]
        else:
            pairs = [(mine, others(mine)), (send, others(send))]
        sent.append(
            [exped(*pair, sent[0][q][:n2] if p else []) for q, pair in enumerate(pairs)]
        )
    parts = []
    for q in range(len(sent[0])):
        far = trade(sent[0][q][n2:], n2), trade(sent[1][q][n2:], n2)
        near = trade(sent[1][q][:n2], 0)
        parts.append(to_planes([*near, *far[0], *far[1]], device, nx))
    if by_core:
        other = lax.ppermute(parts[0], "dens", swap)
        mine = jnp.arange(2)[:, None, None, None] == core[0]
        bary = jnp.where(mine, parts[0][None], other[None])
        return bary.reshape(planes, nx, ny), scalings[None]
    return jnp.concatenate(parts, 0), scalings[None]


def solution(mesh):
    return jax.shard_map(
        local,
        mesh=mesh,
        in_specs=(P("dens", "sp", None, None), P("dens"), P()),
        out_specs=(P("sp", None, None), P("dens", "sp", None, None)),
        check_vma=False,
    )
```
